32 devices in a mesh: sky: 2 (over x), seg: 16 (over z, y, core).
Axes of the slice: x: 2, y: 2, z: 4, core: 2. Of those that a mesh axis runs over, the one named last changes fastest.
Arguments:
- strain_series: bfloat16 [32, 2, 65536], P(('sky', 'seg')), parts along dimension 0, may hold values from -6 to 6
- antenna: float32 [32, 2, 65536], P(('sky', 'seg')), parts along dimension 0, may hold values from -160 to 160, as said below
- drift: int32 [32, 6], P(('sky', 'seg')), parts along dimension 0, may hold values from -2 to 2
- tracks: int32 [64, 16], replicated, may hold values from 0 to 5
Outputs:
- track_stat: float32 [128, 65536], P('sky', 'seg'), parts along dimension 0
The draws below stay inside these ranges and needn't reach their ends.
There are 2 independent parts, one for each index of `sky`. The reference program is written for one: setup_inputs(seed, part) draws one part's arguments, and reference() takes and returns one part's arrays. A program takes and returns all parts, laid end to end along the dimension named above; an argument that names none is the same for every part. Nothing has to cross between parts.
Inputs may be any that keep to these rules, and one draw needn't show every extreme that they name: `antenna`: row 0 holds the a weights, row 1 the b weights of each segment.
All inputs are finite; a program needn't handle non-finite values.
Results may differ from the reference program's by a relative error of at most 0.0015.
Values sent between devices are 32-bit elements; how exact they have to be, the bound alone decides.
A program may use at most 192 MiB of HBM per device.

```python
import math
import jax
import jax.numpy as jnp
from jax import lax

NBIN = 65536
DFT_ROWS = 256
BLK = 128
DMAX = 2
KCOH = 6
NTRACK = 64
NSEG = 16


def draw_antenna(key, part):
    key_noise = jax.random.fold_in(key, 11)
    key_corr = jax.random.fold_in(key, 12)
    key_level = jax.random.fold_in(key, 13)
    noise = jnp.clip(jax.random.normal(key_noise, (NSEG, 2, NBIN), jnp.float32), -5.0, 5.0)
    levels = jax.random.uniform(key_level, (NSEG, 16), jnp.float32, 0.0, math.log(10.0))
    corr = jax.random.uniform(key_corr, (NSEG, 1), jnp.float32, -0.995, 0.995)
    envelope = jnp.repeat(jnp.exp(levels), NBIN // 16, axis=1)
    first = envelope * noise[:, 0]
    second = envelope * (corr * noise[:, 0] + jnp.sqrt(1.0 - corr * corr) * noise[:, 1])
    return jnp.stack([first, second], 1)


def plant(array, key, low, largest):
    longest = array.shape.index(max(array.shape))
    spots = []
    for shift in (0, 1):
        where = [jax.random.randint(jax.random.fold_in(key, axis), (), 0, length) for axis, length in enumerate(array.shape)]
        where[longest] = (where[longest] + shift) % array.shape[longest]
        spots.append(tuple(where))
    return array.at[spots[0]].set(low).at[spots[1]].set(largest)


def steps_of(stream_key, dims, shards, smallest, high):
    loudness, own = 1.0, jax.random.fold_in(stream_key, 6)
    for axis_at, shards_of in shards:
        heights = jnp.exp(jax.random.uniform(jax.random.fold_in(own, axis_at), (shards_of,), jnp.float32, smallest / len(shards), high / len(shards)))
        loudness = loudness * jnp.repeat(heights, dims[axis_at] // shards_of).reshape([-1 if axis == axis_at else 1 for axis in range(len(dims))])
    return loudness


def bell_draw(rng, dims, scale, most, cuts=(), kind=jnp.bfloat16):
    result = scale * jax.random.normal(rng, dims, jnp.float32)
    if cuts:
        result = result * steps_of(rng, dims, cuts, -0.22, 0.18)
    return jnp.clip(result, -most, most).astype(kind)


def setup_inputs(seed: int = 0, part: int = 0) -> dict:
    keys = jax.random.split(jax.random.key(seed), 5)
    part_splits = jax.random.split(jax.random.fold_in(keys[4], part), 5)
    strain_series = bell_draw(part_splits[0], (NSEG, 2, NBIN), 1.0, 6.0, ((0, 16),))
    antenna = draw_antenna(jax.random.fold_in(jax.random.fold_in(keys[4], part), 71), part)
    drift = plant(jax.random.randint(part_splits[2], (NSEG, KCOH), 0 - DMAX, DMAX + 1), jax.random.fold_in(part_splits[2], 1), 0 - DMAX, DMAX).astype(jnp.int32)
    tracks = plant(jax.random.randint(keys[3], (NTRACK, NSEG), 0, KCOH), jax.random.fold_in(keys[3], 1), 0, KCOH - 1).astype(jnp.int32)
    return {"strain_series": strain_series, "antenna": antenna, "drift": drift, "tracks": tracks}


chirp_step = 3.0
tiny_eps = 1e-6


def section_tables(points, first_rows):
    second_rows = points // first_rows
    outer_index = jnp.arange(first_rows, dtype=jnp.int32)
    inner_index = jnp.arange(second_rows, dtype=jnp.int32)
    first_angle = (2.0 * math.pi / first_rows) * ((outer_index[:, None] * outer_index[None, :]) % first_rows).astype(jnp.float32)
    cos_one, sin_one = jnp.cos(first_angle), jnp.sin(first_angle)
    left_table = jnp.stack([jnp.stack([cos_one, sin_one]), jnp.stack([-sin_one, cos_one])]).astype(jnp.bfloat16)
    second_angle = (2.0 * math.pi / second_rows) * ((inner_index[:, None] * inner_index[None, :]) % second_rows).astype(jnp.float32)
    cos_two, sin_two = jnp.cos(second_angle), jnp.sin(second_angle)
    right_table = jnp.stack([jnp.stack([cos_two, -sin_two]), jnp.stack([sin_two, cos_two])]).astype(jnp.bfloat16)
    twist_angle = (2.0 * math.pi / points) * ((outer_index[:, None] * inner_index[None, :]) % points).astype(jnp.float32)
    return left_table, right_table, jnp.cos(twist_angle), jnp.sin(twist_angle)


def coherent_stat(series, weights, left_table, right_table, twist_cos, twist_sin):
    seg_rows = series.shape[0]
    points = series.shape[2]
    first_rows = left_table.shape[2]
    second_rows = points // first_rows
    position = jnp.arange(points, dtype=jnp.float32) / points
    chirp_rate = (jnp.arange(KCOH, dtype=jnp.float32) - (KCOH - 1) / 2.0) * chirp_step
    phases = (2.0 * math.pi) * chirp_rate[:, None] * (position * position)[None, :]
    phase_cos, phase_sin = jnp.cos(phases), jnp.sin(phases)
    series_real = series[:, 0].astype(jnp.float32)[:, None, :]
    series_imag = series[:, 1].astype(jnp.float32)[:, None, :]
    demod_real = series_real * phase_cos + series_imag * phase_sin
    demod_imag = series_imag * phase_cos - series_real * phase_sin
    weight_a = weights[:, 0][:, None, :]
    weight_b = weights[:, 1][:, None, :]
    with_a = jnp.stack([weight_a * demod_real, weight_a * demod_imag], 2)
    with_b = jnp.stack([weight_b * demod_real, weight_b * demod_imag], 2)
    weighted = jnp.stack([with_a, with_b], 2).astype(jnp.bfloat16)
    weighted = weighted.reshape(seg_rows * KCOH * 2, 2, first_rows, second_rows)
    section_one = jnp.einsum('oikn,binm->bokm', left_table.astype(jnp.float32), weighted.astype(jnp.float32))
    one_real, one_imag = section_one[:, 0], section_one[:, 1]
    twisted_real = one_real * twist_cos + one_imag * twist_sin
    twisted_imag = one_imag * twist_cos - one_real * twist_sin
    middle = jnp.stack([twisted_real, twisted_imag], 1).astype(jnp.bfloat16)
    spectra = jnp.einsum('bikm,ioml->bolk', middle.astype(jnp.float32), right_table.astype(jnp.float32))
    spectra = spectra.reshape(seg_rows, KCOH, 2, 2, points)
    a_real, a_imag = spectra[:, :, 0, 0], spectra[:, :, 0, 1]
    b_real, b_imag = spectra[:, :, 1, 0], spectra[:, :, 1, 1]
    weight_aa = jnp.mean(weights[:, 0] * weights[:, 0], axis=-1) + tiny_eps
    weight_bb = jnp.mean(weights[:, 1] * weights[:, 1], axis=-1) + tiny_eps
    weight_ab = jnp.mean(weights[:, 0] * weights[:, 1], axis=-1)
    determinant = jnp.maximum(weight_aa * weight_bb - weight_ab * weight_ab, 0.1 * weight_aa * weight_bb)
    energy = (weight_bb[:, None, None] * (a_real * a_real + a_imag * a_imag)
              + weight_aa[:, None, None] * (b_real * b_real + b_imag * b_imag)
              - 2.0 * weight_ab[:, None, None] * (a_real * b_real + a_imag * b_imag))
    return energy / (points * determinant[:, None, None])


def drift_blocks(padded, offsets, extent, amount):
    summed = jnp.zeros(padded.shape[:-2] + (amount, padded.shape[-1]), padded.dtype)
    for offset in range(-extent, extent + 1):
        window = padded[..., extent - offset:extent - offset + amount, :]
        summed = summed + jnp.where((offsets == offset)[..., None, None], window, 0.0)
    return summed


def reference(strain_series, antenna, drift, tracks):
    left_table, right_table, twist_cos, twist_sin = section_tables(NBIN, DFT_ROWS)

    def one_segment(item):
        series, weights = item
        return coherent_stat(series[None], weights[None], left_table, right_table, twist_cos, twist_sin)[0]

    stats = lax.map(one_segment, (strain_series, antenna))
    blocks = stats.reshape(NSEG, KCOH, NBIN // BLK, BLK)
    padded = jnp.pad(blocks, ((0, 0), (0, 0), (DMAX, DMAX), (0, 0)))
    moved = drift_blocks(padded, drift, DMAX, NBIN // BLK).reshape(NSEG, KCOH, NBIN)
    levels = jnp.arange(KCOH, dtype=jnp.int32)
    pick = (tracks[:, :, None] == levels[None, None, :]).astype(jnp.float32)
    summed = jnp.einsum('jsk,skf->jf', pick, moved, precision=lax.Precision.HIGHEST)
    return summed / NSEG
```

```python
import functools
import math

import jax
import jax.numpy as jnp
import numpy as np
from jax import lax
from jax.experimental import pallas as pl
from jax.experimental.pallas import tpu as pltpu
from jax.sharding import PartitionSpec as P

DFT_ROWS = 256
BLK = 128
DMAX = 2
KCOH = 6
PAD = 8

chirp_step = 3.0
tiny_eps = 1e-06


def dft_table(rows):
    index = np.arange(rows, dtype=np.int64)
    angle = np.float32(2.0 * math.pi / rows) * (index[:, None] * index[None, :] % rows).astype(np.float32)
    cos, sin = np.cos(angle), np.sin(angle)
    return np.block([[cos, sin], [-sin, cos]]).astype(jnp.bfloat16)


def twist_table(points, first_rows):
    second_rows = points // first_rows
    outer = np.arange(first_rows, dtype=np.int64)
    inner = np.arange(second_rows, dtype=np.int64)
    angle = np.float32(2.0 * math.pi / points) * (outer[:, None] * inner[None, :] % points).astype(np.float32)
    return np.stack([np.cos(angle), np.sin(angle)]).astype(np.float32)


def chirp_table(points, first_rows):
    position = np.arange(points, dtype=np.float32) / np.float32(points)
    rate = (np.arange(KCOH // 2, KCOH, dtype=np.float32) - np.float32((KCOH - 1) / 2.0)) * np.float32(chirp_step)
    phases = (np.float32(2.0 * math.pi) * rate)[:, None] * (position * position)[None, :]
    both = np.stack([np.cos(phases), np.sin(phases)], 1).astype(np.float32)
    return both.reshape(KCOH // 2, 2, first_rows, points // first_rows)


def kernel(
    count, drift_ref, series_ref, antenna_ref, chirp_ref, twist_ref, first_ref, second_ref, pick_ref, out_ref,
    weighted, spread, middle, padded, send, recv, send_sem, recv_sem,
):
    _, first_rows, second_rows = series_ref.shape
    rows = second_rows // count
    points = first_rows * second_rows
    halves = first_rows // BLK
    sky = lax.axis_index("sky")
    me = lax.axis_index("seg")

    barrier = pltpu.get_barrier_semaphore()

    def greet(step, carry):
        pl.semaphore_signal(
            barrier, inc=1, device_id=(sky, lax.rem(me + step, count)), device_id_type=pl.DeviceIdType.MESH
        )
        return carry

    lax.fori_loop(1, count, greet, 0)

    weight_a, weight_b = antenna_ref[0], antenna_ref[1]
    total = lambda value: jnp.sum(jnp.sum(value, axis=0, keepdims=True), axis=1, keepdims=True)
    aa = total(weight_a * weight_a) / points + tiny_eps
    bb = total(weight_b * weight_b) / points + tiny_eps
    ab = total(weight_a * weight_b) / points
    scale = 1.0 / (points * jnp.maximum(aa * bb - ab * ab, 0.1 * aa * bb))
    coef_a, coef_b, coef_ab = bb * scale, aa * scale, 2.0 * ab * scale

    for half in range(halves):
        padded[half, :PAD] = jnp.zeros((PAD, BLK), jnp.float32)
        padded[half, PAD + second_rows :] = jnp.zeros((PAD, BLK), jnp.float32)

    pl.semaphore_wait(barrier, count - 1)

    def one_rate(k, carry):
        upper = k >= KCOH // 2
        level = jnp.where(upper, k - KCOH // 2, KCOH // 2 - 1 - k)
        sign = jnp.where(upper, 1.0, -1.0)
        chirp_cos = chirp_ref[level, 0]
        chirp_sin = chirp_ref[level, 1] * sign
        real, imag = series_ref[0].astype(jnp.float32), series_ref[1].astype(jnp.float32)
        demod_real = real * chirp_cos + imag * chirp_sin
        demod_imag = imag * chirp_cos - real * chirp_sin
        for which in range(2):
            weight = antenna_ref[which]
            columns = slice(which * second_rows, (which + 1) * second_rows)
            weighted[:first_rows, columns] = (weight * demod_real).astype(jnp.bfloat16)
            weighted[first_rows:, columns] = (weight * demod_imag).astype(jnp.bfloat16)
        spread[...] = jnp.dot(first_ref[...], weighted[...], preferred_element_type=jnp.float32)
        twist_cos, twist_sin = twist_ref[0], twist_ref[1]
        for which in range(2):
            columns = slice(which * second_rows, (which + 1) * second_rows)
            one_real, one_imag = spread[:first_rows, columns], spread[first_rows:, columns]
            lines = slice(which * first_rows, (which + 1) * first_rows)
            middle[lines, :second_rows] = (one_real * twist_cos + one_imag * twist_sin).astype(jnp.bfloat16)
            middle[lines, second_rows:] = (one_imag * twist_cos - one_real * twist_sin).astype(jnp.bfloat16)
        spread[...] = lax.dot_general(
            second_ref[...], middle[...], (((1,), (1,)), ((), ())), preferred_element_type=jnp.float32
        )
        for half in range(halves):
            at_a = slice(half * BLK, (half + 1) * BLK)
            at_b = slice(first_rows + half * BLK, first_rows + (half + 1) * BLK)
            a_real, a_imag = spread[:second_rows, at_a], spread[second_rows:, at_a]
            b_real, b_imag = spread[:second_rows, at_b], spread[second_rows:, at_b]
            padded[half, PAD : PAD + second_rows] = (
                coef_a * (a_real * a_real + a_imag * a_imag)
                + coef_b * (b_real * b_real + b_imag * b_imag)
                - coef_ab * (a_real * b_real + a_imag * b_imag)
            )
        shift = drift_ref[0, k]

        def place(peer, inner):
            for half in range(halves):
                block = half - shift + halves * PAD
                source = lax.rem(block, halves)
                start = lax.div(block, halves) + rows * peer
                send[k, peer, :, half * BLK : (half + 1) * BLK] = padded[source, pl.ds(start, rows), :]
            return inner

        lax.fori_loop(0, count, place, 0)

        def ship(step, inner):
            peer = lax.rem(me + step, count)
            pltpu.make_async_remote_copy(
                src_ref=send.at[k, peer],
                dst_ref=recv.at[k, me],
                send_sem=send_sem.at[k],
                recv_sem=recv_sem.at[k],
                device_id=(sky, peer),
                device_id_type=pl.DeviceIdType.MESH,
            ).start()
            return inner

        lax.fori_loop(count // 2, count, ship, 0)
        lax.fori_loop(1, count // 2, ship, 0)
        pltpu.make_async_copy(send.at[k, me], recv.at[k, me], recv_sem.at[k]).start()
        return carry

    lax.fori_loop(0, KCOH, one_rate, 0)

    for k in range(KCOH):
        pltpu.make_async_copy(recv.at[k], recv.at[k], recv_sem.at[k]).wait()

    pick = pick_ref[...]
    for row in range(rows):
        value = recv[:, :, row, :].reshape(KCOH * count, first_rows)
        high = value.astype(jnp.bfloat16)
        low = (value - high.astype(jnp.float32)).astype(jnp.bfloat16)
        out_ref[:, row * first_rows : (row + 1) * first_rows] = jnp.dot(
            pick, jnp.concatenate([high, low], 0), preferred_element_type=jnp.float32
        )

    for k in range(KCOH):
        part = send.at[k, pl.ds(0, count - 1)]
        pltpu.make_async_copy(part, part, send_sem.at[k]).wait()


def local(count, strain_series, antenna, drift, tracks):
    points = strain_series.shape[2]
    first_rows, second_rows = DFT_ROWS, points // DFT_ROWS
    segments = tracks.shape[1]
    rows = second_rows // count
    levels = jnp.arange(KCOH, dtype=jnp.int32)
    pick = (tracks[:, None, :] == levels[None, :, None]).astype(jnp.bfloat16)
    pick = pick.reshape(tracks.shape[0], KCOH * segments)
    vmem = pl.BlockSpec(memory_space=pltpu.VMEM)
    summed = pl.pallas_call(
        functools.partial(kernel, count),
        out_shape=jax.ShapeDtypeStruct((tracks.shape[0], points // count), jnp.float32),
        in_specs=[pl.BlockSpec(memory_space=pltpu.SMEM)] + [vmem] * 7,
        out_specs=vmem,
        scratch_shapes=[
            pltpu.VMEM((2 * first_rows, 2 * second_rows), jnp.bfloat16),
            pltpu.VMEM((2 * max(first_rows, second_rows), 2 * max(first_rows, second_rows)), jnp.float32),
            pltpu.VMEM((2 * first_rows, 2 * second_rows), jnp.bfloat16),
            pltpu.VMEM((first_rows // BLK, second_rows + 2 * PAD, BLK), jnp.float32),
            pltpu.VMEM((KCOH, count, rows, first_rows), jnp.float32),
            pltpu.VMEM((KCOH, count, rows, first_rows), jnp.float32),
            pltpu.SemaphoreType.DMA((KCOH,)),
            pltpu.SemaphoreType.DMA((KCOH,)),
        ],
        compiler_params=pltpu.CompilerParams(
            collective_id=0, has_side_effects=True, vmem_limit_bytes=60 << 20
        ),
    )(
        drift,
        strain_series.reshape(2, first_rows, second_rows),
        antenna.reshape(2, first_rows, second_rows),
        jnp.asarray(chirp_table(points, first_rows)),
        jnp.asarray(twist_table(points, first_rows)),
        jnp.asarray(dft_table(first_rows)),
        jnp.asarray(dft_table(second_rows)),
        jnp.concatenate([pick, pick], 1),
    )
    return summed / segments


def solution(mesh):
    return jax.shard_map(
        functools.partial(local, mesh.shape["seg"]),
        mesh=mesh,
        in_specs=(
            P(("sky", "seg"), None, None),
            P(("sky", "seg"), None, None),
            P(("sky", "seg"), None),
            P(),
        ),
        out_specs=P("sky", "seg"),
        check_vma=False,
    )
```

```python
import functools
import math

import jax
import jax.numpy as jnp
import numpy as np
from jax import lax
from jax.experimental import pallas as pl
from jax.experimental.pallas import tpu as pltpu
from jax.sharding import PartitionSpec as P

DFT_ROWS = 256
BLK = 128
DMAX = 2
KCOH = 6
PAD = 8

chirp_step = 3.0
tiny_eps = 1e-06


def dft_table(rows):
    index = np.arange(rows, dtype=np.int64)
    angle = np.float32(2.0 * math.pi / rows) * (index[:, None] * index[None, :] % rows).astype(np.float32)
    cos, sin = np.cos(angle), np.sin(angle)
    return np.block([[cos, sin], [-sin, cos]]).astype(jnp.bfloat16)


def twist_table(points, first_rows):
    second_rows = points // first_rows
    outer = np.arange(first_rows, dtype=np.int64)
    inner = np.arange(second_rows, dtype=np.int64)
    angle = np.float32(2.0 * math.pi / points) * (outer[:, None] * inner[None, :] % points).astype(np.float32)
    return np.stack([np.cos(angle), np.sin(angle)]).astype(np.float32)


def chirp_table(points, first_rows):
    position = np.arange(points, dtype=np.float32) / np.float32(points)
    rate = (np.arange(KCOH // 2, KCOH, dtype=np.float32) - np.float32((KCOH - 1) / 2.0)) * np.float32(chirp_step)
    phases = (np.float32(2.0 * math.pi) * rate)[:, None] * (position * position)[None, :]
    both = np.stack([np.cos(phases), np.sin(phases)], 1).astype(np.float32)
    return both.reshape(KCOH // 2, 2, first_rows, points // first_rows)


def kernel(
    count, drift_ref, series_ref, antenna_ref, chirp_ref, twist_ref, first_ref, second_ref, tracks_ref, out_ref,
    strain, weights, weighted, spread, middle, padded, send, recv, send_sem, recv_sem,
):
    _, first_rows, second_rows = strain.shape
    rows = second_rows // count
    points = first_rows * second_rows
    halves = first_rows // BLK
    sky = lax.axis_index("sky")
    me = lax.axis_index("seg")

    barrier = pltpu.get_barrier_semaphore()

    def greet(step, carry):
        pl.semaphore_signal(
            barrier, inc=1, device_id=(sky, lax.rem(me + step, count)), device_id_type=pl.DeviceIdType.MESH
        )
        return carry

    lax.fori_loop(1, count, greet, 0)

    pieces = second_rows // BLK
    for which in range(2):
        for piece in range(pieces):
            lanes = slice(piece * BLK, (piece + 1) * BLK)
            lines = pl.ds(piece, first_rows, stride=pieces)
            strain[which, :, lanes] = series_ref[lines, which, :]
            weights[which, :, lanes] = antenna_ref[lines, which, :]

    weight_a, weight_b = weights[0], weights[1]
    total = lambda value: jnp.sum(jnp.sum(value, axis=0, keepdims=True), axis=1, keepdims=True)
    aa = total(weight_a * weight_a) / points + tiny_eps
    bb = total(weight_b * weight_b) / points + tiny_eps
    ab = total(weight_a * weight_b) / points
    scale = 1.0 / (points * jnp.maximum(aa * bb - ab * ab, 0.1 * aa * bb))
    coef_a, coef_b, coef_ab = bb * scale, aa * scale, 2.0 * ab * scale

    for half in range(halves):
        padded[half, :PAD] = jnp.zeros((PAD, BLK), jnp.float32)
        padded[half, PAD + second_rows :] = jnp.zeros((PAD, BLK), jnp.float32)

    pl.semaphore_wait(barrier, count - 1)

    def one_rate(k, carry):
        upper = k >= KCOH // 2
        level = jnp.where(upper, k - KCOH // 2, KCOH // 2 - 1 - k)
        sign = jnp.where(upper, 1.0, -1.0)
        chirp_cos = chirp_ref[level, 0]
        chirp_sin = chirp_ref[level, 1] * sign
        real, imag = strain[0], strain[1]
        demod_real = real * chirp_cos + imag * chirp_sin
        demod_imag = imag * chirp_cos - real * chirp_sin
        for which in range(2):
            weight = weights[which]
            columns = slice(which * second_rows, (which + 1) * second_rows)
            weighted[:first_rows, columns] = (weight * demod_real).astype(jnp.bfloat16)
            weighted[first_rows:, columns] = (weight * demod_imag).astype(jnp.bfloat16)
        spread[...] = jnp.dot(first_ref[...], weighted[...], preferred_element_type=jnp.float32)
        twist_cos, twist_sin = twist_ref[0], twist_ref[1]
        for which in range(2):
            columns = slice(which * second_rows, (which + 1) * second_rows)
            one_real, one_imag = spread[:first_rows, columns], spread[first_rows:, columns]
            lines = slice(which * first_rows, (which + 1) * first_rows)
            middle[lines, :second_rows] = (one_real * twist_cos + one_imag * twist_sin).astype(jnp.bfloat16)
            middle[lines, second_rows:] = (one_imag * twist_cos - one_real * twist_sin).astype(jnp.bfloat16)
        spread[...] = lax.dot_general(
            second_ref[...], middle[...], (((1,), (1,)), ((), ())), preferred_element_type=jnp.float32
        )
        for half in range(halves):
            at_a = slice(half * BLK, (half + 1) * BLK)
            at_b = slice(first_rows + half * BLK, first_rows + (half + 1) * BLK)
            a_real, a_imag = spread[:second_rows, at_a], spread[second_rows:, at_a]
            b_real, b_imag = spread[:second_rows, at_b], spread[second_rows:, at_b]
            padded[half, PAD : PAD + second_rows] = (
                coef_a * (a_real * a_real + a_imag * a_imag)
                + coef_b * (b_real * b_real + b_imag * b_imag)
                - coef_ab * (a_real * b_real + a_imag * b_imag)
            )
        shift = drift_ref[0, k]

        def place(peer, inner):
            for half in range(halves):
                block = half - shift + halves * PAD
                source = lax.rem(block, halves)
                start = lax.div(block, halves) + rows * peer
                send[k, peer, :, half * BLK : (half + 1) * BLK] = padded[source, pl.ds(start, rows), :]
            return inner

        lax.fori_loop(0, count, place, 0)

        def ship(step, inner):
            peer = lax.rem(me + step, count)
            pltpu.make_async_remote_copy(
                src_ref=send.at[k, peer],
                dst_ref=recv.at[k, me],
                send_sem=send_sem.at[k],
                recv_sem=recv_sem.at[k],
                device_id=(sky, peer),
                device_id_type=pl.DeviceIdType.MESH,
            ).start()
            return inner

        lax.fori_loop(count // 2, count, ship, 0)
        lax.fori_loop(1, count // 2, ship, 0)
        pltpu.make_async_copy(send.at[k, me], recv.at[k, me], recv_sem.at[k]).start()
        return carry

    lax.fori_loop(0, KCOH, one_rate, 0)

    out_ref[...] = jnp.zeros_like(out_ref)

    def collect(k, carry):
        pltpu.make_async_copy(recv.at[k], recv.at[k], recv_sem.at[k]).wait()
        pick = jnp.where(tracks_ref[...] == k, 1.0, 0.0).astype(jnp.bfloat16)
        for row in range(rows):
            value = recv[k, :, row, :]
            high = value.astype(jnp.bfloat16)
            low = (value - high.astype(jnp.float32)).astype(jnp.bfloat16)
            columns = slice(row * first_rows, (row + 1) * first_rows)
            out_ref[:, columns] += jnp.dot(pick, high, preferred_element_type=jnp.float32) + jnp.dot(
                pick, low, preferred_element_type=jnp.float32
            )
        return carry

    lax.fori_loop(0, KCOH, collect, 0)

    for k in range(KCOH):
        part = send.at[k, pl.ds(0, count - 1)]
        pltpu.make_async_copy(part, part, send_sem.at[k]).wait()


def local(count, strain_series, antenna, drift, tracks):
    points = strain_series.shape[2]
    first_rows, second_rows = DFT_ROWS, points // DFT_ROWS
    segments = tracks.shape[1]
    rows = second_rows // count
    blocked = lambda array: array.reshape(2, points // BLK, BLK).transpose(1, 0, 2)
    vmem = pl.BlockSpec(memory_space=pltpu.VMEM)
    summed = pl.pallas_call(
        functools.partial(kernel, count),
        out_shape=jax.ShapeDtypeStruct((tracks.shape[0], points // count), jnp.float32),
        in_specs=[pl.BlockSpec(memory_space=pltpu.SMEM)] + [vmem] * 7,
        out_specs=vmem,
        scratch_shapes=[
            pltpu.VMEM((2, first_rows, second_rows), jnp.float32),
            pltpu.VMEM((2, first_rows, second_rows), jnp.float32),
            pltpu.VMEM((2 * first_rows, 2 * second_rows), jnp.bfloat16),
            pltpu.VMEM((2 * max(first_rows, second_rows), 2 * max(first_rows, second_rows)), jnp.float32),
            pltpu.VMEM((2 * first_rows, 2 * second_rows), jnp.bfloat16),
            pltpu.VMEM((first_rows // BLK, second_rows + 2 * PAD, BLK), jnp.float32),
            pltpu.VMEM((KCOH, count, rows, first_rows), jnp.float32),
            pltpu.VMEM((KCOH, count, rows, first_rows), jnp.float32),
            pltpu.SemaphoreType.DMA((KCOH,)),
            pltpu.SemaphoreType.DMA((KCOH,)),
        ],
        compiler_params=pltpu.CompilerParams(
            collective_id=0, has_side_effects=True, vmem_limit_bytes=60 << 20
        ),
    )(
        drift,
        blocked(strain_series.astype(jnp.float32)),
        blocked(antenna),
        jnp.asarray(chirp_table(points, first_rows)),
        jnp.asarray(twist_table(points, first_rows)),
        jnp.asarray(dft_table(first_rows)),
        jnp.asarray(dft_table(second_rows)),
        tracks,
    )
    return summed / segments


def solution(mesh):
    return jax.shard_map(
        functools.partial(local, mesh.shape["seg"]),
        mesh=mesh,
        in_specs=(
            P(("sky", "seg"), None, None),
            P(("sky", "seg"), None, None),
            P(("sky", "seg"), None),
            P(),
        ),
        out_specs=P("sky", "seg"),
        check_vma=False,
    )
```

```python
import functools
import math

import jax
import jax.numpy as jnp
import numpy as np
from jax import lax
from jax.experimental import pallas as pl
from jax.experimental.pallas import tpu as pltpu
from jax.sharding import PartitionSpec as P

DFT_ROWS = 256
BLK = 128
DMAX = 2
KCOH = 6
PAD = 8

chirp_step = 3.0
tiny_eps = 1e-06


def dft_table(rows):
    index = np.arange(rows, dtype=np.int64)
    angle = np.float32(2.0 * math.pi / rows) * (index[:, None] * index[None, :] % rows).astype(np.float32)
    cos, sin = np.cos(angle), np.sin(angle)
    return np.block([[cos, sin], [-sin, cos]]).astype(jnp.bfloat16)


def twist_table(points, first_rows):
    second_rows = points // first_rows
    outer = np.arange(first_rows, dtype=np.int64)
    inner = np.arange(second_rows, dtype=np.int64)
    angle = np.float32(2.0 * math.pi / points) * (outer[:, None] * inner[None, :] % points).astype(np.float32)
    return np.stack([np.cos(angle), np.sin(angle)]).astype(np.float32)


def chirp_table(points, first_rows):
    position = np.arange(points, dtype=np.float32) / np.float32(points)
    rate = (np.arange(KCOH // 2, KCOH, dtype=np.float32) - np.float32((KCOH - 1) / 2.0)) * np.float32(chirp_step)
    phases = (np.float32(2.0 * math.pi) * rate)[:, None] * (position * position)[None, :]
    both = np.stack([np.cos(phases), np.sin(phases)], 1).astype(np.float32)
    return both.reshape(KCOH // 2, 2, first_rows, points // first_rows)


def kernel(
    count, drift_ref, series_ref, antenna_ref, chirp_ref, twist_ref, first_ref, second_ref, tracks_ref, out_ref,
    strain, weights, weighted, spread, middle, padded, send, recv, send_sem, recv_sem,
):
    _, first_rows, second_rows = strain.shape
    rows = second_rows // count
    points = first_rows * second_rows
    halves = first_rows // BLK
    sky = lax.axis_index("sky")
    me = lax.axis_index("seg")

    barrier = pltpu.get_barrier_semaphore()

    def greet(step, carry):
        pl.semaphore_signal(
            barrier, inc=1, device_id=(sky, lax.rem(me + step, count)), device_id_type=pl.DeviceIdType.MESH
        )
        return carry

    lax.fori_loop(1, count, greet, 0)

    pieces = second_rows // BLK
    for which in range(2):
        for piece in range(pieces):
            lanes = slice(piece * BLK, (piece + 1) * BLK)
            lines = pl.ds(piece, first_rows, stride=pieces)
            strain[which, :, lanes] = series_ref[lines, which, :]
            weights[which, :, lanes] = antenna_ref[lines, which, :]

    weight_a, weight_b = weights[0], weights[1]
    total = lambda value: jnp.sum(jnp.sum(value, axis=0, keepdims=True), axis=1, keepdims=True)
    aa = total(weight_a * weight_a) / points + tiny_eps
    bb = total(weight_b * weight_b) / points + tiny_eps
    ab = total(weight_a * weight_b) / points
    scale = 1.0 / (points * jnp.maximum(aa * bb - ab * ab, 0.1 * aa * bb))
    coef_a, coef_b, coef_ab = bb * scale, aa * scale, 2.0 * ab * scale

    for half in range(halves):
        padded[half, :PAD] = jnp.zeros((PAD, BLK), jnp.float32)
        padded[half, PAD + second_rows :] = jnp.zeros((PAD, BLK), jnp.float32)

    pl.semaphore_wait(barrier, count - 1)

    def one_rate(k, carry):
        upper = k >= KCOH // 2
        level = jnp.where(upper, k - KCOH // 2, KCOH // 2 - 1 - k)
        sign = jnp.where(upper, 1.0, -1.0)
        chirp_cos = chirp_ref[level, 0]
        chirp_sin = chirp_ref[level, 1] * sign
        real, imag = strain[0], strain[1]
        demod_real = real * chirp_cos + imag * chirp_sin
        demod_imag = imag * chirp_cos - real * chirp_sin
        for which in range(2):
            weight = weights[which]
            columns = slice(which * second_rows, (which + 1) * second_rows)
            weighted[:first_rows, columns] = (weight * demod_real).astype(jnp.bfloat16)
            weighted[first_rows:, columns] = (weight * demod_imag).astype(jnp.bfloat16)
        spread[...] = jnp.dot(first_ref[...], weighted[...], preferred_element_type=jnp.float32)
        twist_cos, twist_sin = twist_ref[0], twist_ref[1]
        for which in range(2):
            columns = slice(which * second_rows, (which + 1) * second_rows)
            one_real, one_imag = spread[:first_rows, columns], spread[first_rows:, columns]
            lines = slice(which * first_rows, (which + 1) * first_rows)
            middle[lines, :second_rows] = (one_real * twist_cos + one_imag * twist_sin).astype(jnp.bfloat16)
            middle[lines, second_rows:] = (one_imag * twist_cos - one_real * twist_sin).astype(jnp.bfloat16)
        spread[...] = lax.dot_general(
            second_ref[...], middle[...], (((1,), (1,)), ((), ())), preferred_element_type=jnp.float32
        )
        for half in range(halves):
            at_a = slice(half * BLK, (half + 1) * BLK)
            at_b = slice(first_rows + half * BLK, first_rows + (half + 1) * BLK)
            a_real, a_imag = spread[:second_rows, at_a], spread[second_rows:, at_a]
            b_real, b_imag = spread[:second_rows, at_b], spread[second_rows:, at_b]
            padded[half, PAD : PAD + second_rows] = (
                coef_a * (a_real * a_real + a_imag * a_imag)
                + coef_b * (b_real * b_real + b_imag * b_imag)
                - coef_ab * (a_real * b_real + a_imag * b_imag)
            )
        shift = drift_ref[0, k]

        def place(peer, inner):
            for half in range(halves):
                block = half - shift + halves * PAD
                source = lax.rem(block, halves)
                start = lax.div(block, halves) + rows * peer
                send[k, peer, :, half * BLK : (half + 1) * BLK] = padded[source, pl.ds(start, rows), :]
            return inner

        lax.fori_loop(0, count, place, 0)

        def ship(step, inner):
            peer = lax.rem(me + step, count)
            pltpu.make_async_remote_copy(
                src_ref=send.at[k, peer],
                dst_ref=recv.at[k, me],
                send_sem=send_sem.at[k],
                recv_sem=recv_sem.at[k],
                device_id=(sky, peer),
                device_id_type=pl.DeviceIdType.MESH,
            ).start()
            return inner

        lax.fori_loop(1, count, ship, 0)
        pltpu.make_async_copy(send.at[k, me], recv.at[k, me], recv_sem.at[k]).start()
        return carry

    lax.fori_loop(0, KCOH, one_rate, 0)

    out_ref[...] = jnp.zeros_like(out_ref)
    add_rows = lambda pick, value: lax.dot_general(
        pick, value, (((0,), (0,)), ((), ())), preferred_element_type=jnp.float32
    )

    def collect(k, carry):
        pltpu.make_async_copy(recv.at[k], recv.at[k], recv_sem.at[k]).wait()
        pick = jnp.where(tracks_ref[...] == k, 1.0, 0.0).astype(jnp.bfloat16)
        for row in range(rows):
            value = recv[k, :, row, :]
            high = value.astype(jnp.bfloat16)
            low = (value - high.astype(jnp.float32)).astype(jnp.bfloat16)
            columns = slice(row * first_rows, (row + 1) * first_rows)
            out_ref[:, columns] += add_rows(pick, high) + add_rows(pick, low)
        return carry

    lax.fori_loop(0, KCOH, collect, 0)

    for k in range(KCOH):
        part = send.at[k, pl.ds(0, count - 1)]
        pltpu.make_async_copy(part, part, send_sem.at[k]).wait()


def local(count, strain_series, antenna, drift, tracks):
    points = strain_series.shape[2]
    first_rows, second_rows = DFT_ROWS, points // DFT_ROWS
    segments = tracks.shape[1]
    rows = second_rows // count
    blocked = lambda array: array.reshape(2, points // BLK, BLK).transpose(1, 0, 2)
    vmem = pl.BlockSpec(memory_space=pltpu.VMEM)
    summed = pl.pallas_call(
        functools.partial(kernel, count),
        out_shape=pltpu.VMEM((tracks.shape[0], points // count), jnp.float32),
        in_specs=[pl.BlockSpec(memory_space=pltpu.SMEM)] + [vmem] * 7,
        out_specs=vmem,
        scratch_shapes=[
            pltpu.VMEM((2, first_rows, second_rows), jnp.float32),
            pltpu.VMEM((2, first_rows, second_rows), jnp.float32),
            pltpu.VMEM((2 * first_rows, 2 * second_rows), jnp.bfloat16),
            pltpu.VMEM((2 * max(first_rows, second_rows), 2 * max(first_rows, second_rows)), jnp.float32),
            pltpu.VMEM((2 * first_rows, 2 * second_rows), jnp.bfloat16),
            pltpu.VMEM((first_rows // BLK, second_rows + 2 * PAD, BLK), jnp.float32),
            pltpu.VMEM((KCOH, count, rows, first_rows), jnp.float32),
            pltpu.VMEM((KCOH, count, rows, first_rows), jnp.float32),
            pltpu.SemaphoreType.DMA((KCOH,)),
            pltpu.SemaphoreType.DMA((KCOH,)),
        ],
        compiler_params=pltpu.CompilerParams(
            collective_id=0, has_side_effects=True, vmem_limit_bytes=60 << 20
        ),
    )(
        drift,
        blocked(strain_series.astype(jnp.float32)),
        blocked(antenna),
        jnp.asarray(chirp_table(points, first_rows)),
        jnp.asarray(twist_table(points, first_rows)),
        jnp.asarray(dft_table(first_rows)),
        jnp.asarray(dft_table(second_rows)),
        tracks.T,
    )
    return summed / segments


def solution(mesh):
    return jax.shard_map(
        functools.partial(local, mesh.shape["seg"]),
        mesh=mesh,
        in_specs=(
            P(("sky", "seg"), None, None),
            P(("sky", "seg"), None, None),
            P(("sky", "seg"), None),
            P(),
        ),
        out_specs=P("sky", "seg"),
        check_vma=False,
    )
```
